32 devices in a mesh: ctx: 16 (over z, x, core), tp: 2 (over y).
Axes of the slice: x: 2, y: 2, z: 4, core: 2. Of those that a mesh axis runs over, the one named last changes fastest.
Arguments:
- inner_input: bfloat16 [2048, 8192], P('ctx', 'tp'), may hold values from -6 to 6
- gate_input: bfloat16 [2048, 8192], P('ctx', 'tp'), may hold values from -6 to 6
- state_inputs: bfloat16 [2, 2048, 1024], P(None, 'ctx', 'tp'), may hold values from -6 to 6
- step_size: float32 [128, 2048], P('tp', 'ctx'), may hold values from 0.5 to 2
- resets: int32 [2048], P('ctx'), may hold values 0 or 1
- decay_rate: float32 [128], P('tp'), may hold values from 0 to 0.04
- skip_gain: float32 [128], P('tp'), may hold values from 0.5 to 1.5
- conv_inner: float32 [4, 8192], P(None, 'tp'), may hold values from -3 to 3
- conv_state: float32 [2, 4, 1024], P(None, None, 'tp'), may hold values from -3 to 3
- norm_gain: float32 [8192], P('tp'), may hold values from 0.5 to 1.5
- out_weight: bfloat16 [8192, 4096], P('tp', 'ctx'), may hold values from -0.0625 to 0.0625
- residual: bfloat16 [2048, 4096], P('ctx', 'tp'), may hold values from -6 to 6
- final_gain: float32 [4096], replicated, may hold values from 0.5 to 1.5
- head_weight: bfloat16 [4096, 65536], P(None, ('ctx', 'tp')), may hold values from -8 to 8
- scored: int32 [128], P('ctx'), may hold values from 0 to 2047, as said below
- targets: int32 [128], replicated, may hold values from 0 to 65535
- policy_logprob: float32 [128], replicated, may hold values from -20 to -10
Outputs:
- ref_logprob: float32 [128], replicated
- token_kl: float32 [128], replicated
The draws below stay inside these ranges and needn't reach their ends.
Inputs may be any that keep to these rules, and one draw needn't show every extreme that they name: `scored`: entries j * 8 to (j + 1) * 8 - 1 are distinct positions in j * 128 to (j + 1) * 128 - 1.
All inputs are finite; a program needn't handle non-finite values. No bound on the sum of `resets` on one device may be relied on, other than what follows from the above.
Results may differ from the reference program's by a relative error of at most 0.00215.
The reference program's roundings to bfloat16 on the way (of `inner_conv`, `normed`, `hidden`, `chosen` and `features`) count: a program that leaves them out, or rounds other values in their place, can miss the bound.
Values may be sent and summed in bfloat16 or wider, within the bound.
A program may use at most 128 MiB of HBM per device.

```python
import math
import jax
import jax.numpy as jnp
from jax import lax

D = 4096
HEADS = 128
HEAD_DIM = 64
STATE = 128
GROUPS = 8
VOCAB = 65536
CONV = 4
SPAN = 128
TOK_DEV = 128
SC_DEV = 8
INNER = 8192
TOKENS = 2048
SCORED = 128


def draw_decay_rate(key, part):
    pick_key, slow_key, fast_key = jax.random.split(key, 3)
    share = 0.5
    slow_heads = jax.random.uniform(pick_key, (HEADS,), jnp.float32) < share
    slow_rate = jnp.exp(jax.random.uniform(slow_key, (HEADS,), jnp.float32, math.log(0.1 / TOKENS), math.log(1.0 / TOKENS)))
    fast_rate = jnp.exp(jax.random.uniform(fast_key, (HEADS,), jnp.float32, math.log(0.02), math.log(0.04)))
    return jnp.where(slow_heads, slow_rate, fast_rate)


def draw_head_weight(key, part):
    base_key = jax.random.fold_in(key, 0)
    weights = jnp.clip(jax.random.normal(base_key, (D, VOCAB), jnp.float32), -6.0, 6.0) * (3.0 / D ** 0.5)
    return weights.astype(jnp.bfloat16)


def draw_scored(key, part):
    blocks = SCORED // SC_DEV

    def one_block(index):
        order = jax.random.permutation(jax.random.fold_in(key, index), TOK_DEV)
        return order[:SC_DEV] + index * TOK_DEV
    return jax.vmap(one_block)(jnp.arange(blocks)).reshape(SCORED).astype(jnp.int32)


def with_ends(entries, own_key, low, top_value):
    longest = entries.shape.index(max(entries.shape))
    spots = []
    for shift in (0, 1):
        where = [jax.random.randint(jax.random.fold_in(own_key, axis), (), 0, length) for axis, length in enumerate(entries.shape)]
        where[longest] = (where[longest] + shift) % entries.shape[longest]
        spots.append(tuple(where))
    return entries.at[spots[0]].set(low).at[spots[1]].set(top_value)


def block_levels(key, shape, cuts, low, high):
    def one(position, parts):
        draws = jax.random.uniform(jax.random.fold_in(jax.random.fold_in(key, 6), position), (parts,), jnp.float32, low / len(cuts), high / len(cuts))
        return jnp.repeat(jnp.exp(draws), shape[position] // parts).reshape((-1,) + (1,) * (len(shape) - position - 1))

    factor_of = one(*cuts[0])
    for cut in cuts[1:]:
        factor_of = factor_of * one(*cut)
    return factor_of


def centred(key, shape, deviation, bound, cuts=(), held_as=jnp.bfloat16):
    factor_of = block_levels(key, shape, cuts, -0.22, 0.18) if cuts else 1.0
    values = jax.random.normal(key, shape, jnp.float32) * deviation * factor_of
    return jnp.minimum(jnp.maximum(values, -bound), bound).astype(held_as)


def setup_inputs(seed: int = 0) -> dict:
    keys = jax.random.split(jax.random.key(seed), 18)
    inner_input = centred(keys[0], (TOKENS, INNER), 1.0, 6.0, ((0, 16), (1, 2)))
    gate_input = centred(keys[1], (TOKENS, INNER), 1.0, 6.0, ((0, 16), (1, 2)))
    state_inputs = centred(keys[2], (2, TOKENS, GROUPS * STATE), 1.0, 6.0, ((1, 16), (2, 2)))
    step_size = jnp.clip(jnp.exp(math.log(2.0) - 1.3862944 * jax.random.uniform(keys[3], (HEADS, TOKENS), jnp.float32) ** block_levels(keys[3], (HEADS, TOKENS), ((0, 2), (1, 16)), -0.2, 0.2)), 0.5, 2.0)
    resets = with_ends((jax.random.randint(keys[4], (TOKENS,), 0, TOKENS // 4) < 1).astype(jnp.int32), jax.random.fold_in(keys[4], 1), 0, 1)
    decay_rate = draw_decay_rate(jax.random.fold_in(keys[17], 71), 0)
    skip_gain = jnp.clip(0.5 + 1.0 * jax.random.uniform(keys[6], (HEADS,), jnp.float32) ** block_levels(keys[6], (HEADS,), ((0, 2),), -0.2, 0.2), 0.5, 1.5)
    conv_inner = centred(keys[7], (CONV, INNER), CONV ** -0.5, 3.0, ((1, 2),), jnp.float32)
    conv_state = centred(keys[8], (2, CONV, GROUPS * STATE), CONV ** -0.5, 3.0, ((2, 2),), jnp.float32)
    norm_gain = jnp.clip(1.0 + 0.1 * jax.random.normal(keys[9], (INNER,), jnp.float32), 0.5, 1.5)
    out_weight = centred(keys[10], (INNER, D), INNER ** -0.5, 0.0625, ((0, 2), (1, 16)))
    residual = centred(keys[11], (TOKENS, D), 1.0, 6.0, ((0, 16), (1, 2)))
    final_gain = jnp.clip(1.0 + 0.1 * jax.random.normal(keys[12], (D,), jnp.float32), 0.5, 1.5)
    head_weight = draw_head_weight(jax.random.fold_in(keys[17], 71), 0)
    scored = draw_scored(jax.random.fold_in(keys[17], 71), 0)
    targets = with_ends(jax.random.randint(keys[15], (SCORED,), 0, VOCAB), jax.random.fold_in(keys[15], 1), 0, VOCAB - 1).astype(jnp.int32)
    policy_logprob = jnp.clip(jax.random.uniform(keys[16], (SCORED,), jnp.float32, -20.0, -10.0), -20.0, -10.0)
    return dict(inner_input=inner_input, gate_input=gate_input, state_inputs=state_inputs, step_size=step_size, resets=resets, decay_rate=decay_rate, skip_gain=skip_gain, conv_inner=conv_inner, conv_state=conv_state, norm_gain=norm_gain, out_weight=out_weight, residual=residual, final_gain=final_gain, head_weight=head_weight, scored=scored, targets=targets, policy_logprob=policy_logprob)


epsilon = 1e-05
precise = lax.Precision.HIGHEST

def causal_filter(stream, kernel, counted):
    kernel_taps = kernel.shape[0]
    rows_total = stream.shape[0]
    values = stream.astype(jnp.float32)
    summed = jnp.zeros_like(values)
    for offset in range(kernel_taps):
        shifted = jnp.concatenate([jnp.zeros((offset, values.shape[1]), jnp.float32), values[:rows_total - offset]], axis=0)
        earlier = jnp.concatenate([jnp.zeros((offset,), counted.dtype), counted[:rows_total - offset]])
        keeping = (counted - earlier == 0).astype(jnp.float32)
        summed = summed + keeping[:, None] * kernel[offset][None, :] * shifted
    return jax.nn.silu(summed).astype(jnp.bfloat16)

def reference(inner_input, gate_input, state_inputs, step_size, resets, decay_rate, skip_gain, conv_inner, conv_state, norm_gain, out_weight, residual, final_gain, head_weight, scored, targets, policy_logprob):
    counted = jnp.cumsum(resets)
    inner_conv = causal_filter(inner_input, conv_inner, counted)
    write_map = causal_filter(state_inputs[0], conv_state[0], counted)
    read_map = causal_filter(state_inputs[1], conv_state[1], counted)
    spans = TOKENS // SPAN
    per_group = HEADS // GROUPS
    values = inner_conv.reshape(spans, SPAN, HEADS, HEAD_DIM).astype(jnp.float32)
    writes = jnp.repeat(write_map.reshape(spans, SPAN, GROUPS, STATE), per_group, axis=2).astype(jnp.float32)
    reads = jnp.repeat(read_map.reshape(spans, SPAN, GROUPS, STATE), per_group, axis=2).astype(jnp.float32)
    steps_blocked = step_size.reshape(HEADS, spans, SPAN).transpose(1, 0, 2)
    segments = resets.reshape(spans, SPAN)
    positions = jnp.arange(SPAN)
    lower = positions[:, None] >= positions[None, :]

    def span_update(states, item):
        value_block, write_block, read_block, step_block, reset_block = item
        cumulated = jnp.cumsum(-decay_rate[:, None] * step_block, axis=1)
        segment = jnp.cumsum(reset_block)
        causal = lower & (segment[:, None] == segment[None, :])
        gaps = cumulated[:, :, None] - cumulated[:, None, :]
        decay_matrix = jnp.where(causal[None], jnp.exp(jnp.where(causal[None], gaps, 0.0)), 0.0)
        scores = jnp.einsum('ihn,jhn->hij', read_block, write_block, precision=precise)
        mixing = scores * decay_matrix * step_block[:, None, :]
        within = jnp.einsum('hij,jhp->ihp', mixing, value_block, precision=precise)
        from_start = jnp.exp(cumulated) * (segment == 0)[None, :]
        across = jnp.einsum('ihn,hpn->ihp', read_block, states, precision=precise) * from_start.T[:, :, None]
        to_end = jnp.exp(cumulated[:, -1:] - cumulated) * (segment == segment[-1])[None, :] * step_block
        weighted = value_block * to_end.T[:, :, None]
        span_decay = jnp.exp(cumulated[:, -1]) * (segment[-1] == 0)
        updated = span_decay[:, None, None] * states + jnp.einsum('jhp,jhn->hpn', weighted, write_block, precision=precise)
        return (updated, within + across)
    empty_state = jnp.zeros((HEADS, HEAD_DIM, STATE), jnp.float32)
    _, outputs = lax.scan(span_update, empty_state, (values, writes, reads, steps_blocked, segments))
    mixed_out = outputs.reshape(TOKENS, HEADS * HEAD_DIM) + jnp.repeat(skip_gain, HEAD_DIM)[None, :] * values.reshape(TOKENS, HEADS * HEAD_DIM)
    gated = mixed_out * jax.nn.silu(gate_input.astype(jnp.float32))
    grouped = gated.reshape(TOKENS, GROUPS, -1)
    inverse_rms = lax.rsqrt(lax.optimization_barrier(jnp.mean(grouped * grouped, axis=2, keepdims=True)) + epsilon)
    normed = ((grouped * inverse_rms).reshape(TOKENS, -1) * norm_gain[None, :]).astype(jnp.bfloat16)
    branch = jnp.dot(normed, out_weight, preferred_element_type=jnp.float32)
    hidden = (residual.astype(jnp.float32) + branch).astype(jnp.bfloat16)
    chosen = hidden[scored]
    squares = lax.optimization_barrier(jnp.sum(jnp.square(chosen.astype(jnp.float32)), axis=1))
    features = (chosen.astype(jnp.float32) * lax.rsqrt(squares / D + epsilon)[:, None] * final_gain[None, :]).astype(jnp.bfloat16)
    logits = jnp.dot(features, head_weight, preferred_element_type=jnp.float32)
    row_top = lax.optimization_barrier(jnp.max(logits, axis=1))
    summed = lax.optimization_barrier(jnp.sum(jnp.exp(logits - row_top[:, None]), axis=1))
    picked = jnp.take_along_axis(logits, targets[:, None], axis=1)[:, 0]
    ref_logprob = picked - row_top - jnp.log(summed)
    token_kl = 0.5 * jnp.square(ref_logprob - policy_logprob)
    return (ref_logprob, token_kl)
```

```python
import functools
import jax
import jax.numpy as jnp
from jax import lax
from jax.experimental import pallas as pl
from jax.experimental.pallas import tpu as pltpu
from jax.sharding import PartitionSpec as P

HEAD_DIM = 64
STATE = 128
EDGE = 16

epsilon = 1e-05
precise = lax.Precision.HIGHEST
MESH = pl.DeviceIdType.MESH
VMEM = pl.BlockSpec(memory_space=pltpu.VMEM)
ANY = pl.BlockSpec(memory_space=pl.ANY)


def remote(src, dst, send, recv, device):
    return pltpu.make_async_remote_copy(
        src_ref=src, dst_ref=dst, send_sem=send, recv_sem=recv, device_id=device, device_id_type=MESH
    )


def greet(devices):
    barrier = pltpu.get_barrier_semaphore()
    for device in devices:
        pl.semaphore_signal(barrier, inc=1, device_id=device, device_id_type=MESH)
    pl.semaphore_wait(barrier, len(devices))


def spread_kernel(n, tp, q_count, z_count, x_ref, s_ref, d_ref, g_ref, m_ref, r_ref,
                  xo, so, do, go, mo, xh, sh, mh, ro,
                  send, recv, own, edge_send, edge_recv, res_send, res_recv):
    c, t = lax.axis_index("ctx"), lax.axis_index("tp")
    z, q = c // q_count, c % q_count
    total = n * tp
    me = c * tp + t
    barrier = pltpu.get_barrier_semaphore()

    def hello(k, carry):
        other = (me + k) % total
        pl.semaphore_signal(
            barrier, inc=1, device_id=(other // tp, other % tp), device_id_type=MESH
        )
        return carry

    lax.fori_loop(1, total, hello, 0)
    pl.semaphore_wait(barrier, total - 1)
    width = xo.shape[2]
    heads = do.shape[1]
    rows = x_ref.shape[0]

    def cols(ref, k, size):
        return ref.at[:, pl.ds(pl.multiple_of(k * size, 128), size)]

    def parts(k):
        return (
            cols(x_ref, k, width),
            s_ref.at[:, :, pl.ds(pl.multiple_of(k * STATE, 128), STATE)],
            d_ref.at[pl.ds(pl.multiple_of(k * heads, 8), heads), :],
            cols(g_ref, k, width),
            m_ref,
        )

    def slots(k):
        return (xo.at[k], so.at[k], do.at[k], go.at[k], mo.at[k])

    started = []
    tail = pl.ds(rows - EDGE, EDGE)
    next_z = jnp.minimum(z + 1, z_count - 1)

    def edges(k, dst_c):
        wide = pl.ds(pl.multiple_of(k * width, 128), width)
        thin = pl.ds(pl.multiple_of(k * STATE, 128), STATE)
        triple = ((x_ref.at[tail, wide], xh), (s_ref.at[:, tail, thin], sh), (m_ref, mh))
        return [
            remote(a, b, edge_send.at[k, i], edge_recv.at[i], (dst_c, t))
            for i, (a, b) in enumerate(triple)
        ]

    sends_edge = (q == q_count - 1) & (z < z_count - 1)
    gets_edge = z > 0
    if z_count > 1:
        @pl.when(sends_edge)
        def _():
            for k in range(q_count):
                for copy in edges(k, (z + 1) * q_count + k):
                    copy.start()

    for d in range(1, q_count):
        k = (q + d) % q_count
        for i, (a, b) in enumerate(zip(parts(k), slots(q))):
            copy = remote(a, b, send.at[d - 1, i], recv.at[d - 1, i], (z * q_count + k, t))
            copy.start()
            started.append(copy)
    per = n // tp

    def res_copy(j, to_t):
        return remote(
            r_ref.at[j], ro.at[c],
            res_send.at[j * tp + to_t], res_recv.at[c], (t * per + j, to_t)
        )

    for j in range(per):
        for to_t in range(tp):
            mine = (t * per + j == c) & (to_t == t)

            @pl.when(jnp.logical_not(mine))
            def _():
                res_copy(j, to_t).start()

            @pl.when(mine)
            def _():
                pltpu.make_async_copy(r_ref.at[j], ro.at[c], res_recv.at[c]).start()
    locals_ = [
        pltpu.make_async_copy(a, b, own.at[i]) for i, (a, b) in enumerate(zip(parts(q), slots(q)))
    ]
    for copy in locals_:
        copy.start()
    for copy in locals_:
        copy.wait()
    for j in range(per):
        for to_t in range(tp):
            mine = (t * per + j == c) & (to_t == t)

            @pl.when(jnp.logical_not(mine))
            def _():
                res_copy(j, to_t).wait_send()
    for k in range(n):
        pltpu.make_async_copy(ro.at[k], ro.at[k], res_recv.at[k]).wait()
    for copy in started:
        copy.wait_send()
    for d in range(1, q_count):
        k = (q + q_count - d) % q_count
        for i, (a, b) in enumerate(zip(parts(q), slots(k))):
            remote(a, b, send.at[d - 1, i], recv.at[d - 1, i], (z * q_count + k, t)).wait_recv()
    if z_count > 1:
        @pl.when(sends_edge)
        def _():
            for k in range(q_count):
                for copy in edges(k, (z + 1) * q_count + k):
                    copy.wait_send()

        @pl.when(gets_edge)
        def _():
            for i, ref in enumerate((xh, sh, mh)):
                pltpu.make_async_copy(ref, ref, edge_recv.at[i]).wait()


def spread(n, tp, q_count, x, s, d, g, m, r):
    z_count = n // q_count
    rows, all_width = x.shape
    width = all_width // q_count
    heads = d.shape[0] // q_count
    block = r.shape[1] * tp // n
    r = r.reshape(r.shape[0], n // tp, block).transpose(1, 0, 2)
    shape = jax.ShapeDtypeStruct
    outs = (
        shape((q_count, rows, width), x.dtype),
        shape((q_count, 2, rows, STATE), s.dtype),
        shape((q_count, heads, rows), d.dtype),
        shape((q_count, g.shape[0], width), g.dtype),
        shape((q_count,) + m.shape, m.dtype),
        shape((EDGE, width), x.dtype),
        shape((2, EDGE, STATE), s.dtype),
        shape(m.shape, m.dtype),
        shape((n,) + r.shape[1:], r.dtype),
    )
    dma = pltpu.SemaphoreType.DMA
    peers = max(q_count - 1, 1)
    return pl.pallas_call(
        functools.partial(spread_kernel, n, tp, q_count, z_count),
        out_shape=outs,
        in_specs=[ANY, ANY, ANY, VMEM, VMEM, VMEM],
        out_specs=[VMEM] * len(outs),
        scratch_shapes=[
            dma((peers, 5)), dma((peers, 5)), dma((5,)), dma((q_count, 3)), dma((3,)),
            dma((n,)), dma((n,)),
        ],
        compiler_params=pltpu.CompilerParams(collective_id=0, has_side_effects=True),
    )(x, s, d, g, m, r)


def exchange_kernel(stride, size, axis, modes, *refs):
    count = len(modes)
    ins, outs = refs[:count], refs[count : 2 * count]
    send, recv, own = refs[2 * count :]
    me = lax.axis_index(axis)
    place = (me // stride) % size

    def device(k):
        other = me + (k - place) * stride
        c, t = lax.axis_index("ctx"), lax.axis_index("tp")
        return (other, t) if axis == "ctx" else (c, other)

    greet([device((place + d) % size) for d in range(1, size)])

    def source(i, k):
        return ins[i].at[k] if modes[i] else ins[i]

    copies = []
    for d in range(1, size):
        k = (place + d) % size
        for i in range(count):
            copy = remote(
                source(i, k), outs[i].at[place], send.at[d - 1, i], recv.at[d - 1, i], device(k)
            )
            copy.start()
            copies.append(copy)
    for i in range(count):
        pltpu.make_async_copy(source(i, place), outs[i].at[place], own.at[i]).start()
    for i in range(count):
        pltpu.make_async_copy(source(i, place), outs[i].at[place], own.at[i]).wait()
    for copy in copies:
        copy.wait_send()
    for d in range(1, size):
        k = (place + size - d) % size
        for i in range(count):
            remote(
                source(i, place), outs[i].at[k], send.at[d - 1, i], recv.at[d - 1, i], device(k)
            ).wait_recv()


def exchange(arrays, modes, stride, size, axis, ident):
    if size == 1:
        return [a if mode else a[None] for a, mode in zip(arrays, modes)]
    outs = [
        jax.ShapeDtypeStruct(a.shape if mode else (size,) + a.shape, a.dtype)
        for a, mode in zip(arrays, modes)
    ]
    dma = pltpu.SemaphoreType.DMA
    count = len(arrays)
    return pl.pallas_call(
        functools.partial(exchange_kernel, stride, size, axis, modes),
        out_shape=outs,
        in_specs=[VMEM] * count,
        out_specs=[VMEM] * count,
        scratch_shapes=[dma((size - 1, count)), dma((size - 1, count)), dma((count,))],
        compiler_params=pltpu.CompilerParams(collective_id=ident, has_side_effects=True),
    )(*arrays)


def tail_kernel(n, tp, q_count, z_count, n_ref, ow_ref, hw_ref, r_ref, g_ref, t_ref, p_ref, out,
                ow, hw, nrm, both, hid, feat, logit, stat, every,
                own, tp_send, tp_recv, st_send, st_recv, *gather_sems):
    c, t = lax.axis_index("ctx"), lax.axis_index("tp")
    z, q = c // q_count, c % q_count
    total = n * tp
    me = c * tp + t
    get_ow = pltpu.make_async_copy(ow_ref, ow, own.at[0])
    get_hw = pltpu.make_async_copy(hw_ref, hw, own.at[1])
    barrier = pltpu.get_barrier_semaphore()

    def device(k):
        return (k // tp, k % tp)

    def hello(d, carry):
        pl.semaphore_signal(
            barrier, inc=1, device_id=device((me + d) % total), device_id_type=MESH
        )
        return carry

    lax.fori_loop(1, total, hello, 0)
    get_ow.start()
    get_hw.start()
    pl.semaphore_wait(barrier, total - 1)
    core_n = 2 if q_count % 2 == 0 else 1
    x_n = q_count // core_n
    x, core = q // core_n, q % core_n

    def at_x(k):
        return (z * q_count + k * core_n + core, t)

    at_core = (z * q_count + x * core_n + (core_n - 1) - core, t)

    def gathered(slot, mine, sems):
        z_send, z_recv, x_send, x_recv, c_send, c_recv = sems
        sent = []

        def push(copy):
            copy.start()
            sent.append(copy)

        def to_x(ref, dst, d):
            for e in range(1, x_n):
                push(remote(ref, dst, x_send.at[e - 1, d], x_recv.at[e - 1, d], at_x((x + e) % x_n)))

        def to_core(ref, dst, e, d):
            if core_n > 1:
                push(remote(ref, dst, c_send.at[e, d], c_recv.at[e, d], at_core))

        home = slot(q, z)
        for d in range(1, z_count):
            push(remote(mine, home, z_send.at[d], z_recv.at[d], (((z + d) % z_count) * q_count + q, t)))
        to_x(mine, home, 0)
        to_core(mine, home, 0, 0)
        for d in range(z_count):
            k = (z + z_count - d) % z_count
            if d:
                here = slot(q, k)
                remote(here, here, z_send.at[d], z_recv.at[d], at_core).wait_recv()
                to_x(here, here, d)
                to_core(here, here, 0, d)
            for e in range(1, x_n):
                here = slot(((x + x_n - e) % x_n) * core_n + core, k)
                remote(here, here, x_send.at[e - 1, d], x_recv.at[e - 1, d], at_core).wait_recv()
                to_core(here, here, e, d)
        if core_n > 1:
            for d in range(z_count):
                k = (z + z_count - d) % z_count
                for e in range(x_n):
                    here = slot(((x + x_n - e) % x_n) * core_n + 1 - core, k)
                    remote(here, here, c_send.at[e, d], c_recv.at[e, d], at_core).wait_recv()
        return sent

    rows = n_ref.shape[0]
    width = n_ref.shape[1]

    def normed_slot(a, b):
        return nrm.at[a, b]

    pending = gathered(normed_slot, n_ref, gather_sems[:6])
    nrm[q, z] = n_ref[...]
    get_ow.wait()
    partial = jnp.zeros(both.shape[1:], jnp.float32)
    for k in range(q_count):
        partial = partial + jnp.dot(
            nrm[k].reshape(z_count * rows, width),
            ow[k * width : (k + 1) * width, :],
            preferred_element_type=jnp.float32,
        )
    both[t] = partial
    tp_copies = []
    for d in range(1, tp):
        copy = remote(both.at[t], both.at[t], tp_send.at[d], tp_recv.at[d], (c, (t + d) % tp))
        copy.start()
        tp_copies.append(copy)
    for d in range(1, tp):
        here = both.at[(t + tp - d) % tp]
        remote(here, here, tp_send.at[d], tp_recv.at[d], (c, (t + d) % tp)).wait_recv()
    summed = both[0]
    for k in range(1, tp):
        summed = summed + both[k]
    hid[q, z] = (r_ref[...].astype(jnp.float32) + summed).astype(jnp.bfloat16)

    def hidden_slot(a, b):
        return hid.at[a, b]

    pending = pending + tp_copies + gathered(hidden_slot, hid.at[q, z], gather_sems[6:])
    block = hid.shape[3]
    all_rows = hid.shape[2]
    squares = jnp.zeros((all_rows, 1), jnp.float32)
    for k in range(z_count):
        for a in range(q_count):
            piece = hid[a, k].astype(jnp.float32)
            squares = squares + jnp.sum(piece * piece, axis=1, keepdims=True)
    inverse = lax.rsqrt(squares / (n * block) + epsilon)
    for k in range(z_count):
        for a in range(q_count):
            first = (k * q_count + a) * block
            span = slice(first, first + block)
            feat[:, span] = (
                hid[a, k].astype(jnp.float32) * inverse * g_ref[:, span]
            ).astype(jnp.bfloat16)
    get_hw.wait()
    vocab = hw.shape[1]
    tile = min(256, vocab)

    def one_tile(i, carry):
        cols = pl.ds(pl.multiple_of(i * tile, 128), tile)
        logit[:, cols] = jnp.dot(feat[...], hw[:, cols], preferred_element_type=jnp.float32)
        return carry

    lax.fori_loop(0, vocab // tile, one_tile, 0)
    values = logit[...]
    top = jnp.max(values, axis=1, keepdims=True)
    added = jnp.sum(jnp.exp(values - top), axis=1, keepdims=True)
    column = t_ref[...] - me * vocab
    places = lax.broadcasted_iota(jnp.int32, values.shape, 1)
    hit = jnp.sum(jnp.where(places == column, values, 0.0), axis=1, keepdims=True)
    lane = lax.broadcasted_iota(jnp.int32, (all_rows, 128), 1)
    packed = jnp.where(lane == 0, top, jnp.where(lane == 1, added, jnp.where(lane == 2, hit, 0.0)))
    turned = packed.T[:8]
    stat[...] = turned

    def go(d, carry):
        remote(
            stat, every.at[me], st_send.at[d], st_recv.at[d], device((me + d) % total)
        ).start()
        return carry

    lax.fori_loop(1, total, go, 0)
    every[me] = turned

    def done(d, carry):
        here = every.at[(me + total - d) % total]
        copy = remote(stat, here, st_send.at[d], st_recv.at[d], device((me + d) % total))
        copy.wait_send()
        copy.wait_recv()
        return carry

    lax.fori_loop(1, total, done, 0)
    for copy in pending:
        copy.wait_send()
    found = every[...]
    tops = found[:, 0, :]
    row_top = jnp.max(tops, axis=0, keepdims=True)
    full = jnp.sum(found[:, 1, :] * jnp.exp(tops - row_top), axis=0, keepdims=True)
    picked = jnp.sum(found[:, 2, :], axis=0, keepdims=True)
    log_prob = picked - row_top - jnp.log(full)
    out[0:1, :] = log_prob
    out[1:2, :] = 0.5 * jnp.square(log_prob - p_ref[...])


def tail(normed, out_weight, head_weight, res, gain, targets, policy, n, tp, q_count, z_count):
    dma = pltpu.SemaphoreType.DMA
    total = n * tp
    rows, width = normed.shape
    all_rows = z_count * rows
    block = out_weight.shape[1]
    core_n = 2 if q_count % 2 == 0 else 1
    x_n = q_count // core_n
    vmem = pltpu.VMEM
    bf16, f32 = jnp.bfloat16, jnp.float32
    e_n = max(x_n - 1, 1)
    sems = [
        dma((z_count,)), dma((z_count,)), dma((e_n, z_count)), dma((e_n, z_count)),
        dma((x_n, z_count)), dma((x_n, z_count)),
    ]
    result = pl.pallas_call(
        functools.partial(tail_kernel, n, tp, q_count, z_count),
        out_shape=jax.ShapeDtypeStruct((2, all_rows), f32),
        in_specs=[VMEM, ANY, ANY, VMEM, VMEM, VMEM, VMEM],
        out_specs=VMEM,
        scratch_shapes=[
            vmem(out_weight.shape, bf16),
            vmem(head_weight.shape, bf16),
            vmem((q_count, z_count, rows, width), bf16),
            vmem((tp, all_rows, block), f32),
            vmem((q_count, z_count, all_rows, block), bf16),
            vmem((all_rows, n * block), bf16),
            vmem((all_rows, head_weight.shape[1]), f32),
            vmem((8, all_rows), f32),
            vmem((total, 8, all_rows), f32),
            dma((2,)), dma((tp,)), dma((tp,)), dma((total,)), dma((total,)),
        ] + sems + sems,
        compiler_params=pltpu.CompilerParams(
            collective_id=3, has_side_effects=True, vmem_limit_bytes=50 * 1024 * 1024
        ),
    )(normed, out_weight, head_weight, res, gain[None], targets[:, None], policy[None])
    return result[0], result[1]


def causal_filter(stream, tail_rows, kernel, keeping):
    kernel_taps = kernel.shape[0]
    rows_here = stream.shape[0]
    padded = jnp.concatenate([tail_rows, stream], axis=0).astype(jnp.float32)
    summed = jnp.zeros((rows_here, stream.shape[1]), jnp.float32)
    for offset in range(kernel_taps):
        anchor = tail_rows.shape[0] - offset
        summed = (
            summed
            + keeping[offset][:, None]
            * kernel[offset][None, :]
            * padded[anchor : anchor + rows_here]
        )
    return jax.nn.silu(summed).astype(jnp.bfloat16)


def body(
    inner_input,
    gate_input,
    state_inputs,
    step_size,
    resets,
    decay_rate,
    skip_gain,
    conv_inner,
    conv_state,
    norm_gain,
    out_weight,
    residual,
    final_gain,
    head_weight,
    scored,
    targets,
    policy_logprob,
):
    f32 = jnp.float32
    n, tp = lax.axis_size("ctx"), lax.axis_size("tp")
    c, t = lax.axis_index("ctx"), lax.axis_index("tp")
    taps = conv_inner.shape[0]
    rows_here = inner_input.shape[0]
    q_count = state_inputs.shape[2] // STATE
    z_count = n // q_count
    z, q = c // q_count, c % q_count
    picked_rows = scored.shape[0]
    local_rows = scored - c * rows_here
    here = jnp.arange(rows_here, dtype=jnp.int32)
    pick = (local_rows[:, None] == here[None, :]).astype(jnp.bfloat16)
    gate_rows = jnp.dot(pick, gate_input, preferred_element_type=f32).astype(jnp.bfloat16)
    res_rows = jnp.dot(pick, residual, preferred_element_type=f32).astype(jnp.bfloat16)
    meta = jnp.zeros((8, rows_here), f32)
    meta = meta.at[0].set(resets.astype(f32))
    meta = meta.at[1, :picked_rows].set(local_rows.astype(f32))
    xs, ss, ds, gs, ms, x_edge, s_edge, m_edge, res_all = spread(
        n, tp, q_count, inner_input, state_inputs, step_size, gate_rows, meta, res_rows
    )
    tokens = q_count * rows_here
    width = xs.shape[2]
    heads = ds.shape[1]
    rows = q_count * picked_rows
    x_raw = xs.reshape(tokens, width)
    s_raw = ss.transpose(1, 0, 2, 3).reshape(2, tokens, STATE)
    steps = ds.transpose(1, 0, 2).reshape(heads, tokens)
    gate = gs.reshape(rows, width)
    flags = ms[:, 0].reshape(tokens)
    spots = ms[:, 1, :picked_rows] + (jnp.arange(q_count) * rows_here).astype(f32)[:, None]
    spots = spots.reshape(rows).astype(jnp.int32)
    has_edge = z > 0
    margin = taps - 1
    x_tail = jnp.where(has_edge, x_edge[EDGE - margin :], jnp.zeros((), x_edge.dtype))
    s_tail = jnp.where(has_edge, s_edge[:, EDGE - margin :], jnp.zeros((), s_edge.dtype))
    f_tail = jnp.where(has_edge, m_edge[0, rows_here - margin :], 0.0)
    clear = 1.0 - jnp.concatenate([f_tail, flags])
    keeping = [jnp.ones((tokens,), f32)]
    for offset in range(1, taps):
        keeping.append(keeping[-1] * clear[margin - offset + 1 : margin - offset + 1 + tokens])
    taps_x = lax.dynamic_slice_in_dim(conv_inner, q * width, width, 1)
    taps_s = lax.dynamic_slice_in_dim(conv_state, q * STATE, STATE, 2)
    rate = lax.dynamic_slice_in_dim(decay_rate, q * heads, heads)
    skip = lax.dynamic_slice_in_dim(skip_gain, q * heads, heads)
    gain = lax.dynamic_slice_in_dim(norm_gain, q * width, width)
    reads = causal_filter(s_raw[1], s_tail[1], taps_s[1], keeping)
    order = jnp.arange(tokens, dtype=jnp.int32)
    one_hot = (spots[:, None] == order[None, :]).astype(jnp.bfloat16)
    reads = jnp.dot(one_hot, reads, preferred_element_type=f32).astype(jnp.bfloat16)
    (all_reads,) = exchange([reads], (False,), q_count, z_count, "ctx", 1)
    values = causal_filter(x_raw, x_tail, taps_x, keeping)
    writes = causal_filter(s_raw[0], s_tail[0], taps_s[0], keeping)
    rises = -rate[:, None] * steps
    below = order[:, None] >= order[None, :]
    cumulated = jnp.dot(rises, below.T.astype(f32), precision=precise)
    segment = jnp.dot(below.astype(f32), flags, precision=precise)
    pick_f = one_hot.astype(f32)
    row_cum = jnp.dot(cumulated, pick_f.T, precision=precise)
    row_seg = jnp.dot(pick_f, segment, precision=precise)
    values_wide = values.astype(f32)
    to_end = jnp.exp(cumulated[:, -1:] - cumulated) * (segment == segment[-1])[None, :] * steps
    weighted = (values_wide.reshape(tokens, heads, HEAD_DIM) * to_end.T[:, :, None]).reshape(
        tokens, width
    )
    state = lax.dot_general(
        writes.astype(f32), weighted, (((0,), (0,)), ((), ())), precision=precise
    )
    plane_decay = jnp.exp(cumulated[:, -1]) * (segment[-1] == 0)
    outgoing = jnp.dot(
        all_reads.reshape(z_count * rows, STATE).astype(f32), state, precision=precise
    ).reshape(z_count, rows, width)
    decay_block = jnp.broadcast_to(
        jnp.pad(plane_decay, (0, -heads % 128))[None, :], (8, heads + -heads % 128)
    )
    far, decays = exchange([outgoing, decay_block], (True, False), q_count, z_count, "ctx", 2)
    causal = (spots[:, None] >= order[None, :]) & (row_seg[:, None] == segment[None, :])
    gaps = row_cum[:, :, None] - cumulated[:, None, :]
    decay = jnp.where(causal[None], jnp.exp(jnp.where(causal[None], gaps, 0.0)), 0.0)
    scores = lax.dot_general(
        reads, writes, (((1,), (1,)), ((), ())), preferred_element_type=f32
    )
    mixing = scores[None] * decay * steps[:, None, :]
    within = jnp.einsum(
        "hrj,jhp->rhp",
        mixing,
        values_wide.reshape(tokens, heads, HEAD_DIM),
        precision=precise,
    )
    decays = decays[:, 0, :heads]
    carried = jnp.zeros((rows, heads, HEAD_DIM), f32)
    for k in range(z_count):
        later = carried * decays[k][None, :, None] + far[k].reshape(rows, heads, HEAD_DIM)
        carried = jnp.where(k < z, later, carried)
    from_start = jnp.exp(row_cum) * (row_seg == 0)[None, :]
    own_values = jnp.dot(one_hot, values, preferred_element_type=f32)
    mixed = (
        within
        + carried * from_start.T[:, :, None]
        + skip[None, :, None] * own_values.reshape(rows, heads, HEAD_DIM)
    ).reshape(rows, width)
    gated = mixed * jax.nn.silu(gate.astype(f32))
    inverse_rms = lax.rsqrt(jnp.mean(gated * gated, axis=1, keepdims=True) + epsilon)
    normed = (gated * inverse_rms * gain[None, :]).astype(jnp.bfloat16)
    res = res_all.reshape(z_count * rows, -1)
    return tail(
        normed, out_weight, head_weight, res, final_gain, targets, policy_logprob,
        n, tp, q_count, z_count,
    )


def solution(mesh):
    return jax.shard_map(
        body,
        mesh=mesh,
        in_specs=(
            P("ctx", "tp"),
            P("ctx", "tp"),
            P(None, "ctx", "tp"),
            P("tp", "ctx"),
            P("ctx"),
            P("tp"),
            P("tp"),
            P(None, "tp"),
            P(None, None, "tp"),
            P("tp"),
            P("tp", "ctx"),
            P("ctx", "tp"),
            P(),
            P(None, ("ctx", "tp")),
            P("ctx"),
            P(),
            P(),
        ),
        out_specs=(P(), P()),
        check_vma=False,
    )
```

```python
import functools
import jax
import jax.numpy as jnp
from jax import lax
from jax.experimental import pallas as pl
from jax.experimental.pallas import tpu as pltpu
from jax.sharding import PartitionSpec as P

HEAD_DIM = 64
STATE = 128
EDGE = 16

epsilon = 1e-05
precise = lax.Precision.HIGHEST
MESH = pl.DeviceIdType.MESH
VMEM = pl.BlockSpec(memory_space=pltpu.VMEM)
ANY = pl.BlockSpec(memory_space=pl.ANY)


def remote(src, dst, send, recv, device):
    return pltpu.make_async_remote_copy(
        src_ref=src, dst_ref=dst, send_sem=send, recv_sem=recv, device_id=device, device_id_type=MESH
    )


def greet(devices):
    barrier = pltpu.get_barrier_semaphore()
    for device in devices:
        pl.semaphore_signal(barrier, inc=1, device_id=device, device_id_type=MESH)
    pl.semaphore_wait(barrier, len(devices))


def spread_kernel(n, tp, q_count, z_count, x_ref, s_ref, d_ref, g_ref, m_ref, r_ref,
                  xo, so, do, go, mo, xh, sh, mh, ro,
                  send, recv, own, edge_send, edge_recv, res_send, res_recv):
    c, t = lax.axis_index("ctx"), lax.axis_index("tp")
    z, q = c // q_count, c % q_count
    total = n * tp
    me = c * tp + t
    barrier = pltpu.get_barrier_semaphore()

    def hello(k, carry):
        other = (me + k) % total
        pl.semaphore_signal(
            barrier, inc=1, device_id=(other // tp, other % tp), device_id_type=MESH
        )
        return carry

    lax.fori_loop(1, total, hello, 0)
    pl.semaphore_wait(barrier, total - 1)
    width = xo.shape[2]
    heads = do.shape[1]
    rows = x_ref.shape[0]

    def cols(ref, k, size):
        return ref.at[:, pl.ds(pl.multiple_of(k * size, 128), size)]

    def parts(k):
        return (
            cols(x_ref, k, width),
            s_ref.at[:, :, pl.ds(pl.multiple_of(k * STATE, 128), STATE)],
            d_ref.at[pl.ds(pl.multiple_of(k * heads, 8), heads), :],
            cols(g_ref, k, width),
            m_ref,
        )

    def slots(k):
        return (xo.at[k], so.at[k], do.at[k], go.at[k], mo.at[k])

    started = []
    tail = pl.ds(rows - EDGE, EDGE)
    next_z = jnp.minimum(z + 1, z_count - 1)

    def edges(k, dst_c):
        wide = pl.ds(pl.multiple_of(k * width, 128), width)
        thin = pl.ds(pl.multiple_of(k * STATE, 128), STATE)
        triple = ((x_ref.at[tail, wide], xh), (s_ref.at[:, tail, thin], sh), (m_ref, mh))
        return [
            remote(a, b, edge_send.at[k, i], edge_recv.at[i], (dst_c, t))
            for i, (a, b) in enumerate(triple)
        ]

    sends_edge = (q == q_count - 1) & (z < z_count - 1)
    gets_edge = z > 0
    if z_count > 1:
        @pl.when(sends_edge)
        def _():
            for k in range(q_count):
                for copy in edges(k, (z + 1) * q_count + k):
                    copy.start()

    for d in range(1, q_count):
        k = (q + d) % q_count
        for i, (a, b) in enumerate(zip(parts(k), slots(q))):
            copy = remote(a, b, send.at[d - 1, i], recv.at[d - 1, i], (z * q_count + k, t))
            copy.start()
            started.append(copy)
    per = n // tp

    def res_copy(j, to_t):
        return remote(
            r_ref.at[j], ro.at[c],
            res_send.at[j * tp + to_t], res_recv.at[c], (t * per + j, to_t)
        )

    for j in range(per):
        for to_t in range(tp):
            mine = (t * per + j == c) & (to_t == t)

            @pl.when(jnp.logical_not(mine))
            def _():
                res_copy(j, to_t).start()

            @pl.when(mine)
            def _():
                pltpu.make_async_copy(r_ref.at[j], ro.at[c], res_recv.at[c]).start()
    locals_ = [
        pltpu.make_async_copy(a, b, own.at[i]) for i, (a, b) in enumerate(zip(parts(q), slots(q)))
    ]
    for copy in locals_:
        copy.start()
    for copy in locals_:
        copy.wait()
    for j in range(per):
        for to_t in range(tp):
            mine = (t * per + j == c) & (to_t == t)

            @pl.when(jnp.logical_not(mine))
            def _():
                res_copy(j, to_t).wait_send()
    for k in range(n):
        pltpu.make_async_copy(ro.at[k], ro.at[k], res_recv.at[k]).wait()
    for copy in started:
        copy.wait_send()
    for d in range(1, q_count):
        k = (q + q_count - d) % q_count
        for i, (a, b) in enumerate(zip(parts(q), slots(k))):
            remote(a, b, send.at[d - 1, i], recv.at[d - 1, i], (z * q_count + k, t)).wait_recv()
    if z_count > 1:
        @pl.when(sends_edge)
        def _():
            for k in range(q_count):
                for copy in edges(k, (z + 1) * q_count + k):
                    copy.wait_send()

        @pl.when(gets_edge)
        def _():
            for i, ref in enumerate((xh, sh, mh)):
                pltpu.make_async_copy(ref, ref, edge_recv.at[i]).wait()


def spread(n, tp, q_count, x, s, d, g, m, r):
    z_count = n // q_count
    rows, all_width = x.shape
    width = all_width // q_count
    heads = d.shape[0] // q_count
    block = r.shape[1] * tp // n
    r = r.reshape(r.shape[0], n // tp, block).transpose(1, 0, 2)
    shape = jax.ShapeDtypeStruct
    outs = (
        shape((q_count, rows, width), x.dtype),
        shape((q_count, 2, rows, STATE), s.dtype),
        shape((q_count, heads, rows), d.dtype),
        shape((q_count, g.shape[0], width), g.dtype),
        shape((q_count,) + m.shape, m.dtype),
        shape((EDGE, width), x.dtype),
        shape((2, EDGE, STATE), s.dtype),
        shape(m.shape, m.dtype),
        shape((n,) + r.shape[1:], r.dtype),
    )
    dma = pltpu.SemaphoreType.DMA
    peers = max(q_count - 1, 1)
    return pl.pallas_call(
        functools.partial(spread_kernel, n, tp, q_count, z_count),
        out_shape=outs,
        in_specs=[ANY, ANY, ANY, VMEM, VMEM, VMEM],
        out_specs=[VMEM] * len(outs),
        scratch_shapes=[
            dma((peers, 5)), dma((peers, 5)), dma((5,)), dma((q_count, 3)), dma((3,)),
            dma((n,)), dma((n,)),
        ],
        compiler_params=pltpu.CompilerParams(collective_id=0, has_side_effects=True),
    )(x, s, d, g, m, r)


def mid_kernel(q_count, z_count, x_ref, xe_ref, s_ref, se_ref, k_ref, d_ref, f_ref, spot_ref,
               gate_ref, tx_ref, ts_ref, rate_ref, skip_ref, gain_ref, out,
               pad_x, pad_s, values, writes, reads, mine_r, all_r, y, far, pd, far_pd, mixed, carried,
               r_send, r_recv, y_send, y_recv, p_send, p_recv):
    f32, bf16 = jnp.float32, jnp.bfloat16
    c, t = lax.axis_index("ctx"), lax.axis_index("tp")
    z, q = c // q_count, c % q_count
    barrier = pltpu.get_barrier_semaphore()

    def peer(d):
        return (((z + d) % z_count) * q_count + q, t)

    for d in range(1, z_count):
        pl.semaphore_signal(barrier, inc=1, device_id=peer(d), device_id_type=MESH)
    tokens, width = values.shape
    piece = tokens // q_count
    heads = d_ref.shape[0]
    rows = mine_r.shape[0]
    taps = tx_ref.shape[0]
    has_edge = (z > 0).astype(f32)
    keep = k_ref[...].T

    def filtered(pad, kernel, start, target):
        total = jnp.zeros((piece, pad.shape[1]), f32)
        for off in range(taps):
            total = total + (
                keep[start : start + piece, off : off + 1]
                * kernel[off : off + 1]
                * pad[EDGE - off + start : EDGE - off + start + piece, :]
            )
        target[start : start + piece, :] = jax.nn.silu(total).astype(bf16)

    thin = pl.ds(pl.multiple_of(q * STATE, 128), STATE)
    for which, target in ((1, reads), (0, writes)):
        edge = se_ref[which].astype(f32)
        pad_s[:EDGE, :] = jnp.where(has_edge > 0.0, edge, 0.0)
        for k in range(q_count):
            pad_s[EDGE + k * piece : EDGE + (k + 1) * piece, :] = s_ref[k, which].astype(f32)
        kernel = ts_ref[which, :, thin]
        for k in range(q_count):
            filtered(pad_s, kernel, k * piece, target)
    spots = spot_ref[...]
    lanes = lax.broadcasted_iota(jnp.int32, (rows, tokens), 1)
    pick_f = jnp.where(spots == lanes, 1.0, 0.0)
    pick = pick_f.astype(bf16)
    mine_r[...] = jnp.dot(pick, reads[...], preferred_element_type=f32).astype(bf16)
    pl.semaphore_wait(barrier, z_count - 1)
    sent = []
    for d in range(1, z_count):
        copy = remote(mine_r, all_r.at[z], r_send.at[d], r_recv.at[d], peer(d))
        copy.start()
        sent.append(copy)
    all_r[z] = mine_r[...]
    wide = pl.ds(pl.multiple_of(q * width, 128), width)
    kernel_x = tx_ref[:, wide]
    pad_x[:EDGE, :] = jnp.where(has_edge > 0.0, xe_ref[...].astype(f32), 0.0)
    for k in range(q_count):
        pad_x[EDGE + k * piece : EDGE + (k + 1) * piece, :] = x_ref[k].astype(f32)
    for k in range(q_count):
        filtered(pad_x, kernel_x, k * piece, values)
    steps = d_ref[...]
    lower = jnp.where(
        lax.broadcasted_iota(jnp.int32, (tokens, tokens), 0)
        <= lax.broadcasted_iota(jnp.int32, (tokens, tokens), 1),
        1.0, 0.0,
    )
    runs = jnp.concatenate([-rate_ref[q] * steps, f_ref[...]], axis=0)
    sums = jnp.dot(runs, lower, precision=precise, preferred_element_type=f32)
    cumulated = sums[:heads]
    segment = sums[heads : heads + 1]
    at_rows = lax.dot_general(
        pick_f, sums, (((1,), (1,)), ((), ())), precision=precise, preferred_element_type=f32
    )
    row_cum = at_rows[:, :heads]
    row_seg = at_rows[:, heads : heads + 1]
    last = cumulated[:, tokens - 1 : tokens]
    last_seg = segment[:, tokens - 1 : tokens]
    to_end = jnp.exp(last - cumulated) * jnp.where(segment == last_seg, 1.0, 0.0) * steps
    spread_heads = jnp.where(
        lax.broadcasted_iota(jnp.int32, (heads, width), 0)
        == lax.broadcasted_iota(jnp.int32, (heads, width), 1) // HEAD_DIM,
        1.0, 0.0,
    )

    def widen(a):
        return jnp.dot(a, spread_heads, precision=precise, preferred_element_type=f32)

    plane = jnp.broadcast_to(jnp.exp(last) * jnp.where(last_seg == 0.0, 1.0, 0.0), (heads, 128))
    pd[...] = widen(plane.T[:8])
    weighted = values[...].astype(f32) * widen(to_end.T)
    state = jnp.dot(
        writes[...].astype(f32).T, weighted, precision=precise, preferred_element_type=f32
    )
    for d in range(1, z_count):
        here = all_r.at[(z + z_count - d) % z_count]
        remote(mine_r, here, r_send.at[d], r_recv.at[d], peer(d)).wait_recv()
    for k in range(z_count):
        y[k] = jnp.dot(
            all_r[k].astype(f32), state, precision=precise, preferred_element_type=f32
        )

    def outgoing(d):
        return (
            remote(y.at[(z + d) % z_count], far.at[z], y_send.at[d], y_recv.at[d], peer(d)),
            remote(pd, far_pd.at[z], p_send.at[d], p_recv.at[d], peer(d)),
        )

    for d in range(1, z_count):
        @pl.when(z + d < z_count)
        def _():
            for copy in outgoing(d):
                copy.start()
    scores = lax.dot_general(
        mine_r[...], writes[...], (((1,), (1,)), ((), ())), preferred_element_type=f32
    )
    causal = (spots >= lanes) & (row_seg == segment)
    half = lax.broadcasted_iota(jnp.int32, (rows, 2 * HEAD_DIM), 1) < HEAD_DIM
    for pair in range(heads // 2):
        mixes = []
        for h in (2 * pair, 2 * pair + 1):
            gaps = row_cum[:, h : h + 1] - cumulated[h : h + 1]
            decay = jnp.where(causal, jnp.exp(jnp.where(causal, gaps, 0.0)), 0.0)
            mixes.append(scores * decay * steps[h : h + 1])
        span = slice(pair * 2 * HEAD_DIM, (pair + 1) * 2 * HEAD_DIM)
        product = jnp.dot(
            jnp.concatenate(mixes, axis=0), values[:, span].astype(f32),
            precision=precise, preferred_element_type=f32,
        )
        mixed[:, span] = jnp.where(half, product[:rows], product[rows:])
    own_values = jnp.dot(pick, values[...], preferred_element_type=f32)
    from_start = jnp.exp(row_cum) * jnp.where(row_seg == 0.0, 1.0, 0.0)
    factors = widen(
        jnp.concatenate([from_start, jnp.broadcast_to(skip_ref[q], (8, heads))], axis=0)
    )
    gate = jax.nn.silu(gate_ref[...].astype(f32))
    carried[...] = jnp.zeros((rows, width), f32)
    for d in range(z_count - 1, 0, -1):
        @pl.when(z - d >= 0)
        def _():
            k = z - d + jnp.where(z - d < 0, z_count, 0)
            here, there = far.at[k], far_pd.at[k]
            remote(here, here, y_send.at[d], y_recv.at[d], peer(d)).wait_recv()
            remote(there, there, p_send.at[d], p_recv.at[d], peer(d)).wait_recv()
            carried[...] = carried[...] * far_pd[k][0:1] + far[k]
    gated = (
        mixed[...] + carried[...] * factors[:rows] + factors[rows : rows + 1] * own_values
    ) * gate
    scale = lax.rsqrt(jnp.mean(gated * gated, axis=1, keepdims=True) + epsilon)
    out[...] = (gated * scale * gain_ref[:, wide]).astype(bf16)
    for copy in sent:
        copy.wait_send()
    for d in range(1, z_count):
        @pl.when(z + d < z_count)
        def _():
            for copy in outgoing(d):
                copy.wait_send()


def middle(xs, x_edge, ss, s_edge, keeps, steps, flags, spots, gate, taps_x, taps_s, rate, skip, gain,
           q_count, z_count):
    f32, bf16 = jnp.float32, jnp.bfloat16
    tokens = steps.shape[1]
    rows, width = gate.shape
    dma, vmem = pltpu.SemaphoreType.DMA, pltpu.VMEM
    return pl.pallas_call(
        functools.partial(mid_kernel, q_count, z_count),
        out_shape=jax.ShapeDtypeStruct((rows, width), bf16),
        in_specs=[VMEM] * 14,
        out_specs=VMEM,
        scratch_shapes=[
            vmem((EDGE + tokens, width), f32),
            vmem((EDGE + tokens, STATE), f32),
            vmem((tokens, width), bf16),
            vmem((tokens, STATE), bf16),
            vmem((tokens, STATE), bf16),
            vmem((rows, STATE), bf16),
            vmem((z_count, rows, STATE), bf16),
            vmem((z_count, rows, width), f32),
            vmem((z_count, rows, width), f32),
            vmem((8, width), f32),
            vmem((z_count, 8, width), f32),
            vmem((rows, width), f32),
            vmem((rows, width), f32),
        ] + [dma((z_count,))] * 6,
        compiler_params=pltpu.CompilerParams(
            collective_id=1, has_side_effects=True, vmem_limit_bytes=50 * 1024 * 1024
        ),
    )(xs, x_edge, ss, s_edge, keeps, steps, flags, spots, gate, taps_x, taps_s, rate, skip, gain)


def tail_kernel(n, tp, q_count, z_count, n_ref, ow_ref, hw_ref, r_ref, g_ref, t_ref, p_ref, out,
                ow, hw, nrm, both, hid, feat, logit, stat, every,
                own, tp_send, tp_recv, st_send, st_recv, *gather_sems):
    c, t = lax.axis_index("ctx"), lax.axis_index("tp")
    z, q = c // q_count, c % q_count
    total = n * tp
    me = c * tp + t
    get_ow = pltpu.make_async_copy(ow_ref, ow, own.at[0])
    get_hw = pltpu.make_async_copy(hw_ref, hw, own.at[1])
    barrier = pltpu.get_barrier_semaphore()

    def device(k):
        return (k // tp, k % tp)

    def hello(d, carry):
        pl.semaphore_signal(
            barrier, inc=1, device_id=device((me + d) % total), device_id_type=MESH
        )
        return carry

    lax.fori_loop(1, total, hello, 0)
    get_ow.start()
    get_hw.start()
    pl.semaphore_wait(barrier, total - 1)
    core_n = 2 if q_count % 2 == 0 else 1
    x_n = q_count // core_n
    x, core = q // core_n, q % core_n

    def at_x(k):
        return (z * q_count + k * core_n + core, t)

    at_core = (z * q_count + x * core_n + (core_n - 1) - core, t)

    def gathered(slot, mine, sems):
        z_send, z_recv, x_send, x_recv, c_send, c_recv = sems
        sent = []

        def push(copy):
            copy.start()
            sent.append(copy)

        def to_x(ref, dst, d):
            for e in range(1, x_n):
                push(remote(ref, dst, x_send.at[e - 1, d], x_recv.at[e - 1, d], at_x((x + e) % x_n)))

        def to_core(ref, dst, e, d):
            if core_n > 1:
                push(remote(ref, dst, c_send.at[e, d], c_recv.at[e, d], at_core))

        home = slot(q, z)
        for d in range(1, z_count):
            push(remote(mine, home, z_send.at[d], z_recv.at[d], (((z + d) % z_count) * q_count + q, t)))
        to_x(mine, home, 0)
        to_core(mine, home, 0, 0)
        for d in range(z_count):
            k = (z + z_count - d) % z_count
            if d:
                here = slot(q, k)
                remote(here, here, z_send.at[d], z_recv.at[d], at_core).wait_recv()
                to_x(here, here, d)
                to_core(here, here, 0, d)
            for e in range(1, x_n):
                here = slot(((x + x_n - e) % x_n) * core_n + core, k)
                remote(here, here, x_send.at[e - 1, d], x_recv.at[e - 1, d], at_core).wait_recv()
                to_core(here, here, e, d)
        if core_n > 1:
            for d in range(z_count):
                k = (z + z_count - d) % z_count
                for e in range(x_n):
                    here = slot(((x + x_n - e) % x_n) * core_n + 1 - core, k)
                    remote(here, here, c_send.at[e, d], c_recv.at[e, d], at_core).wait_recv()
        return sent

    rows = n_ref.shape[0]
    width = n_ref.shape[1]

    def normed_slot(a, b):
        return nrm.at[a, b]

    pending = gathered(normed_slot, n_ref, gather_sems[:6])
    nrm[q, z] = n_ref[...]
    get_ow.wait()
    partial = jnp.zeros(both.shape[1:], jnp.float32)
    for k in range(q_count):
        partial = partial + jnp.dot(
            nrm[k].reshape(z_count * rows, width),
            ow[k * width : (k + 1) * width, :],
            preferred_element_type=jnp.float32,
        )
    both[t] = partial
    tp_copies = []
    for d in range(1, tp):
        copy = remote(both.at[t], both.at[t], tp_send.at[d], tp_recv.at[d], (c, (t + d) % tp))
        copy.start()
        tp_copies.append(copy)
    for d in range(1, tp):
        here = both.at[(t + tp - d) % tp]
        remote(here, here, tp_send.at[d], tp_recv.at[d], (c, (t + d) % tp)).wait_recv()
    summed = both[0]
    for k in range(1, tp):
        summed = summed + both[k]
    hid[q, z] = (r_ref[...].astype(jnp.float32) + summed).astype(jnp.bfloat16)

    def hidden_slot(a, b):
        return hid.at[a, b]

    pending = pending + tp_copies + gathered(hidden_slot, hid.at[q, z], gather_sems[6:])
    block = hid.shape[3]
    all_rows = hid.shape[2]
    squares = jnp.zeros((all_rows, 1), jnp.float32)
    for k in range(z_count):
        for a in range(q_count):
            piece = hid[a, k].astype(jnp.float32)
            squares = squares + jnp.sum(piece * piece, axis=1, keepdims=True)
    inverse = lax.rsqrt(squares / (n * block) + epsilon)
    for k in range(z_count):
        for a in range(q_count):
            first = (k * q_count + a) * block
            span = slice(first, first + block)
            feat[:, span] = (
                hid[a, k].astype(jnp.float32) * inverse * g_ref[:, span]
            ).astype(jnp.bfloat16)
    get_hw.wait()
    vocab = hw.shape[1]
    tile = min(256, vocab)

    def one_tile(i, carry):
        cols = pl.ds(pl.multiple_of(i * tile, 128), tile)
        logit[:, cols] = jnp.dot(feat[...], hw[:, cols], preferred_element_type=jnp.float32)
        return carry

    lax.fori_loop(0, vocab // tile, one_tile, 0)
    values = logit[...]
    top = jnp.max(values, axis=1, keepdims=True)
    added = jnp.sum(jnp.exp(values - top), axis=1, keepdims=True)
    column = t_ref[...] - me * vocab
    places = lax.broadcasted_iota(jnp.int32, values.shape, 1)
    hit = jnp.sum(jnp.where(places == column, values, 0.0), axis=1, keepdims=True)
    lane = lax.broadcasted_iota(jnp.int32, (all_rows, 128), 1)
    packed = jnp.where(lane == 0, top, jnp.where(lane == 1, added, jnp.where(lane == 2, hit, 0.0)))
    turned = packed.T[:8]
    stat[...] = turned

    def go(d, carry):
        remote(
            stat, every.at[me], st_send.at[d], st_recv.at[d], device((me + d) % total)
        ).start()
        return carry

    lax.fori_loop(1, total, go, 0)
    every[me] = turned

    def done(d, carry):
        here = every.at[(me + total - d) % total]
        copy = remote(stat, here, st_send.at[d], st_recv.at[d], device((me + d) % total))
        copy.wait_send()
        copy.wait_recv()
        return carry

    lax.fori_loop(1, total, done, 0)
    for copy in pending:
        copy.wait_send()
    found = every[...]
    tops = found[:, 0, :]
    row_top = jnp.max(tops, axis=0, keepdims=True)
    full = jnp.sum(found[:, 1, :] * jnp.exp(tops - row_top), axis=0, keepdims=True)
    picked = jnp.sum(found[:, 2, :], axis=0, keepdims=True)
    log_prob = picked - row_top - jnp.log(full)
    out[0:1, :] = log_prob
    out[1:2, :] = 0.5 * jnp.square(log_prob - p_ref[...])


def tail(normed, out_weight, head_weight, res, gain, targets, policy, n, tp, q_count, z_count):
    dma = pltpu.SemaphoreType.DMA
    total = n * tp
    rows, width = normed.shape
    all_rows = z_count * rows
    block = out_weight.shape[1]
    core_n = 2 if q_count % 2 == 0 else 1
    x_n = q_count // core_n
    vmem = pltpu.VMEM
    bf16, f32 = jnp.bfloat16, jnp.float32
    e_n = max(x_n - 1, 1)
    sems = [
        dma((z_count,)), dma((z_count,)), dma((e_n, z_count)), dma((e_n, z_count)),
        dma((x_n, z_count)), dma((x_n, z_count)),
    ]
    result = pl.pallas_call(
        functools.partial(tail_kernel, n, tp, q_count, z_count),
        out_shape=jax.ShapeDtypeStruct((2, all_rows), f32),
        in_specs=[VMEM, ANY, ANY, VMEM, VMEM, VMEM, VMEM],
        out_specs=VMEM,
        scratch_shapes=[
            vmem(out_weight.shape, bf16),
            vmem(head_weight.shape, bf16),
            vmem((q_count, z_count, rows, width), bf16),
            vmem((tp, all_rows, block), f32),
            vmem((q_count, z_count, all_rows, block), bf16),
            vmem((all_rows, n * block), bf16),
            vmem((all_rows, head_weight.shape[1]), f32),
            vmem((8, all_rows), f32),
            vmem((total, 8, all_rows), f32),
            dma((2,)), dma((tp,)), dma((tp,)), dma((total,)), dma((total,)),
        ] + sems + sems,
        compiler_params=pltpu.CompilerParams(
            collective_id=3, has_side_effects=True, vmem_limit_bytes=50 * 1024 * 1024
        ),
    )(normed, out_weight, head_weight, res, gain[None], targets[:, None], policy[None])
    return result[0], result[1]


def body(
    inner_input,
    gate_input,
    state_inputs,
    step_size,
    resets,
    decay_rate,
    skip_gain,
    conv_inner,
    conv_state,
    norm_gain,
    out_weight,
    residual,
    final_gain,
    head_weight,
    scored,
    targets,
    policy_logprob,
):
    f32 = jnp.float32
    n, tp = lax.axis_size("ctx"), lax.axis_size("tp")
    c, t = lax.axis_index("ctx"), lax.axis_index("tp")
    taps = conv_inner.shape[0]
    rows_here = inner_input.shape[0]
    q_count = state_inputs.shape[2] // STATE
    z_count = n // q_count
    z, q = c // q_count, c % q_count
    picked_rows = scored.shape[0]
    local_rows = scored - c * rows_here
    here = jnp.arange(rows_here, dtype=jnp.int32)
    pick = (local_rows[:, None] == here[None, :]).astype(jnp.bfloat16)
    gate_rows = jnp.dot(pick, gate_input, preferred_element_type=f32).astype(jnp.bfloat16)
    res_rows = jnp.dot(pick, residual, preferred_element_type=f32).astype(jnp.bfloat16)
    meta = jnp.zeros((8, rows_here), f32)
    meta = meta.at[0].set(resets.astype(f32))
    meta = meta.at[1, :picked_rows].set(local_rows.astype(f32))
    xs, ss, ds, gs, ms, x_edge, s_edge, m_edge, res_all = spread(
        n, tp, q_count, inner_input, state_inputs, step_size, gate_rows, meta, res_rows
    )
    tokens = q_count * rows_here
    width = xs.shape[2]
    heads = ds.shape[1]
    rows = q_count * picked_rows
    steps = ds.transpose(1, 0, 2).reshape(heads, tokens)
    gate = gs.reshape(rows, width)
    flags = ms[:, 0].reshape(tokens)
    spots = ms[:, 1, :picked_rows] + (jnp.arange(q_count) * rows_here).astype(f32)[:, None]
    spots = spots.reshape(rows, 1).astype(jnp.int32)
    margin = taps - 1
    f_tail = jnp.where(z > 0, m_edge[0, rows_here - margin :], 0.0)
    clear = 1.0 - jnp.concatenate([f_tail, flags])
    keeping = [jnp.ones((tokens,), f32)]
    for offset in range(1, taps):
        keeping.append(keeping[-1] * clear[margin - offset + 1 : margin - offset + 1 + tokens])
    keeps = jnp.pad(jnp.stack(keeping), ((0, -taps % 8), (0, 0)))
    normed = middle(
        xs, x_edge, ss, s_edge, keeps, steps, jnp.broadcast_to(flags[None], (8, tokens)), spots, gate,
        conv_inner, conv_state, decay_rate.reshape(q_count, heads, 1),
        skip_gain.reshape(q_count, 1, heads), norm_gain[None], q_count, z_count,
    )
    res = res_all.reshape(z_count * rows, -1)
    return tail(
        normed, out_weight, head_weight, res, final_gain, targets, policy_logprob,
        n, tp, q_count, z_count,
    )


def solution(mesh):
    return jax.shard_map(
        body,
        mesh=mesh,
        in_specs=(
            P("ctx", "tp"),
            P("ctx", "tp"),
            P(None, "ctx", "tp"),
            P("tp", "ctx"),
            P("ctx"),
            P("tp"),
            P("tp"),
            P(None, "tp"),
            P(None, None, "tp"),
            P("tp"),
            P("tp", "ctx"),
            P("ctx", "tp"),
            P(),
            P(None, ("ctx", "tp")),
            P("ctx"),
            P(),
            P(),
        ),
        out_specs=(P(), P()),
        check_vma=False,
    )
```

```python
import functools
import jax
import jax.numpy as jnp
from jax import lax
from jax.experimental import pallas as pl
from jax.experimental.pallas import tpu as pltpu
from jax.sharding import PartitionSpec as P

HEAD_DIM = 64
STATE = 128
EDGE = 16

epsilon = 1e-05
precise = lax.Precision.HIGHEST
MESH = pl.DeviceIdType.MESH
VMEM = pl.BlockSpec(memory_space=pltpu.VMEM)
ANY = pl.BlockSpec(memory_space=pl.ANY)


def remote(src, dst, send, recv, device):
    return pltpu.make_async_remote_copy(
        src_ref=src, dst_ref=dst, send_sem=send, recv_sem=recv, device_id=device, device_id_type=MESH
    )


def greet(devices):
    barrier = pltpu.get_barrier_semaphore()
    for device in devices:
        pl.semaphore_signal(barrier, inc=1, device_id=device, device_id_type=MESH)
    pl.semaphore_wait(barrier, len(devices))


def spread_kernel(n, tp, q_count, z_count, x_ref, s_ref, d_ref, g_ref, m_ref, r_ref,
                  xo, so, do, go, mo, xh, sh, mh, ro,
                  send, recv, own, edge_send, edge_recv, res_send, res_recv):
    c, t = lax.axis_index("ctx"), lax.axis_index("tp")
    z, q = c // q_count, c % q_count
    total = n * tp
    me = c * tp + t
    barrier = pltpu.get_barrier_semaphore()

    def hello(k, carry):
        other = (me + k) % total
        pl.semaphore_signal(
            barrier, inc=1, device_id=(other // tp, other % tp), device_id_type=MESH
        )
        return carry

    lax.fori_loop(1, total, hello, 0)
    pl.semaphore_wait(barrier, total - 1)
    width = xo.shape[2]
    heads = do.shape[1]
    rows = x_ref.shape[0]

    def cols(ref, k, size):
        return ref.at[:, pl.ds(pl.multiple_of(k * size, 128), size)]

    def parts(k):
        return (
            cols(x_ref, k, width),
            s_ref.at[:, :, pl.ds(pl.multiple_of(k * STATE, 128), STATE)],
            d_ref.at[pl.ds(pl.multiple_of(k * heads, 8), heads), :],
            cols(g_ref, k, width),
            m_ref,
        )

    def slots(k):
        return (xo.at[k], so.at[k], do.at[k], go.at[k], mo.at[k])

    started = []
    tail = pl.ds(rows - EDGE, EDGE)
    next_z = jnp.minimum(z + 1, z_count - 1)

    def edges(k, dst_c):
        wide = pl.ds(pl.multiple_of(k * width, 128), width)
        thin = pl.ds(pl.multiple_of(k * STATE, 128), STATE)
        triple = ((x_ref.at[tail, wide], xh), (s_ref.at[:, tail, thin], sh), (m_ref, mh))
        return [
            remote(a, b, edge_send.at[k, i], edge_recv.at[i], (dst_c, t))
            for i, (a, b) in enumerate(triple)
        ]

    sends_edge = (q == q_count - 1) & (z < z_count - 1)
    gets_edge = z > 0
    if z_count > 1:
        @pl.when(sends_edge)
        def _():
            for k in range(q_count):
                for copy in edges(k, (z + 1) * q_count + k):
                    copy.start()

    for d in range(1, q_count):
        k = (q + d) % q_count
        for i, (a, b) in enumerate(zip(parts(k), slots(q))):
            copy = remote(a, b, send.at[d - 1, i], recv.at[d - 1, i], (z * q_count + k, t))
            copy.start()
            started.append(copy)
    per = n // tp

    def res_copy(j, to_t):
        return remote(
            r_ref.at[j], ro.at[c],
            res_send.at[j * tp + to_t], res_recv.at[c], (t * per + j, to_t)
        )

    for j in range(per):
        for to_t in range(tp):
            mine = (t * per + j == c) & (to_t == t)

            @pl.when(jnp.logical_not(mine))
            def _():
                res_copy(j, to_t).start()

            @pl.when(mine)
            def _():
                pltpu.make_async_copy(r_ref.at[j], ro.at[c], res_recv.at[c]).start()
    locals_ = [
        pltpu.make_async_copy(a, b, own.at[i]) for i, (a, b) in enumerate(zip(parts(q), slots(q)))
    ]
    for copy in locals_:
        copy.start()
    for copy in locals_:
        copy.wait()
    for j in range(per):
        for to_t in range(tp):
            mine = (t * per + j == c) & (to_t == t)

            @pl.when(jnp.logical_not(mine))
            def _():
                res_copy(j, to_t).wait_send()
    for k in range(n):
        pltpu.make_async_copy(ro.at[k], ro.at[k], res_recv.at[k]).wait()
    for copy in started:
        copy.wait_send()
    for d in range(1, q_count):
        k = (q + q_count - d) % q_count
        for i, (a, b) in enumerate(zip(parts(q), slots(k))):
            remote(a, b, send.at[d - 1, i], recv.at[d - 1, i], (z * q_count + k, t)).wait_recv()
    if z_count > 1:
        @pl.when(sends_edge)
        def _():
            for k in range(q_count):
                for copy in edges(k, (z + 1) * q_count + k):
                    copy.wait_send()

        @pl.when(gets_edge)
        def _():
            for i, ref in enumerate((xh, sh, mh)):
                pltpu.make_async_copy(ref, ref, edge_recv.at[i]).wait()


def spread(n, tp, q_count, x, s, d, g, m, r):
    z_count = n // q_count
    rows, all_width = x.shape
    width = all_width // q_count
    heads = d.shape[0] // q_count
    block = r.shape[1] * tp // n
    r = r.reshape(r.shape[0], n // tp, block).transpose(1, 0, 2)
    shape = jax.ShapeDtypeStruct
    outs = (
        shape((q_count, rows, width), x.dtype),
        shape((q_count, 2, rows, STATE), s.dtype),
        shape((q_count, heads, rows), d.dtype),
        shape((q_count, g.shape[0], width), g.dtype),
        shape((q_count,) + m.shape, m.dtype),
        shape((EDGE, width), x.dtype),
        shape((2, EDGE, STATE), s.dtype),
        shape(m.shape, m.dtype),
        shape((n,) + r.shape[1:], r.dtype),
    )
    dma = pltpu.SemaphoreType.DMA
    peers = max(q_count - 1, 1)
    return pl.pallas_call(
        functools.partial(spread_kernel, n, tp, q_count, z_count),
        out_shape=outs,
        in_specs=[ANY, ANY, ANY, VMEM, VMEM, VMEM],
        out_specs=[VMEM] * len(outs),
        scratch_shapes=[
            dma((peers, 5)), dma((peers, 5)), dma((5,)), dma((q_count, 3)), dma((3,)),
            dma((n,)), dma((n,)),
        ],
        compiler_params=pltpu.CompilerParams(collective_id=0, has_side_effects=True),
    )(x, s, d, g, m, r)


def staged(kernel, skip, count, shapes):
    def run(*refs):
        ins, rest, held, sems = (
            refs[:count], refs[count : -len(shapes) - 1], refs[-len(shapes) - 1 : -1], refs[-1]
        )
        held = iter(held)
        views, copies = [], []
        for i, ref in enumerate(ins):
            if i in skip:
                views.append(ref)
                continue
            local = next(held)
            copy = pltpu.make_async_copy(ref, local, sems.at[len(copies)])
            copy.start()
            copies.append(copy)
            views.append(local)
        for copy in copies:
            copy.wait()
        kernel(*views, *rest)

    extra = [pltpu.VMEM(a.shape, a.dtype) for a in shapes]
    return run, extra + [pltpu.SemaphoreType.DMA((len(shapes),))]


def mid_kernel(q_count, z_count, x_ref, xe_ref, s_ref, se_ref, k_ref, d_ref, f_ref, spot_ref,
               gate_ref, tx_ref, ts_ref, rate_ref, skip_ref, gain_ref, out,
               pad_x, pad_s, values, writes, reads, mine_r, all_r, y, far, pd, far_pd, mixed, carried,
               r_send, r_recv, y_send, y_recv, p_send, p_recv):
    f32, bf16 = jnp.float32, jnp.bfloat16
    c, t = lax.axis_index("ctx"), lax.axis_index("tp")
    z, q = c // q_count, c % q_count
    barrier = pltpu.get_barrier_semaphore()

    def peer(d):
        return (((z + d) % z_count) * q_count + q, t)

    for d in range(1, z_count):
        pl.semaphore_signal(barrier, inc=1, device_id=peer(d), device_id_type=MESH)
    tokens, width = values.shape
    piece = tokens // q_count
    heads = d_ref.shape[1]
    rows = mine_r.shape[0]
    taps = tx_ref.shape[0]
    has_edge = (z > 0).astype(f32)
    keep = k_ref[...].T

    def filtered(pad, kernel, start, target):
        total = jnp.zeros((piece, pad.shape[1]), f32)
        for off in range(taps):
            total = total + (
                keep[start : start + piece, off : off + 1]
                * kernel[off : off + 1]
                * pad[EDGE - off + start : EDGE - off + start + piece, :]
            )
        target[start : start + piece, :] = jax.nn.silu(total).astype(bf16)

    thin = pl.ds(pl.multiple_of(q * STATE, 128), STATE)
    for which, target in ((1, reads), (0, writes)):
        edge = se_ref[which].astype(f32)
        pad_s[:EDGE, :] = jnp.where(has_edge > 0.0, edge, 0.0)
        for k in range(q_count):
            pad_s[EDGE + k * piece : EDGE + (k + 1) * piece, :] = s_ref[k, which].astype(f32)
        kernel = ts_ref[which, :, thin]
        for k in range(q_count):
            filtered(pad_s, kernel, k * piece, target)
    spots = spot_ref[...]
    lanes = lax.broadcasted_iota(jnp.int32, (rows, tokens), 1)
    pick_f = jnp.where(spots == lanes, 1.0, 0.0)
    pick = pick_f.astype(bf16)
    mine_r[...] = jnp.dot(pick, reads[...], preferred_element_type=f32).astype(bf16)
    pl.semaphore_wait(barrier, z_count - 1)
    sent = []
    for d in range(1, z_count):
        copy = remote(mine_r, all_r.at[z], r_send.at[d], r_recv.at[d], peer(d))
        copy.start()
        sent.append(copy)
    all_r[z] = mine_r[...]
    wide = pl.ds(pl.multiple_of(q * width, 128), width)
    kernel_x = tx_ref[:, wide]
    pad_x[:EDGE, :] = jnp.where(has_edge > 0.0, xe_ref[...].astype(f32), 0.0)
    for k in range(q_count):
        pad_x[EDGE + k * piece : EDGE + (k + 1) * piece, :] = x_ref[k].astype(f32)
    for k in range(q_count):
        filtered(pad_x, kernel_x, k * piece, values)
    steps = jnp.concatenate([d_ref[k] for k in range(q_count)], axis=1)
    lower = jnp.where(
        lax.broadcasted_iota(jnp.int32, (tokens, tokens), 0)
        <= lax.broadcasted_iota(jnp.int32, (tokens, tokens), 1),
        1.0, 0.0,
    )
    runs = jnp.concatenate([-rate_ref[q] * steps, f_ref[...]], axis=0)
    sums = jnp.dot(runs, lower, precision=precise, preferred_element_type=f32)
    cumulated = sums[:heads]
    segment = sums[heads : heads + 1]
    at_rows = lax.dot_general(
        pick_f, sums, (((1,), (1,)), ((), ())), precision=precise, preferred_element_type=f32
    )
    row_cum = at_rows[:, :heads]
    row_seg = at_rows[:, heads : heads + 1]
    last = cumulated[:, tokens - 1 : tokens]
    last_seg = segment[:, tokens - 1 : tokens]
    to_end = jnp.exp(last - cumulated) * jnp.where(segment == last_seg, 1.0, 0.0) * steps
    spread_heads = jnp.where(
        lax.broadcasted_iota(jnp.int32, (heads, width), 0)
        == lax.broadcasted_iota(jnp.int32, (heads, width), 1) // HEAD_DIM,
        1.0, 0.0,
    )

    def widen(a):
        return jnp.dot(a, spread_heads, precision=precise, preferred_element_type=f32)

    plane = jnp.broadcast_to(jnp.exp(last) * jnp.where(last_seg == 0.0, 1.0, 0.0), (heads, 128))
    pd[...] = widen(plane.T[:8])
    weighted = values[...].astype(f32) * widen(to_end.T)
    state = jnp.dot(
        writes[...].astype(f32).T, weighted, precision=precise, preferred_element_type=f32
    )
    for d in range(1, z_count):
        here = all_r.at[(z + z_count - d) % z_count]
        remote(mine_r, here, r_send.at[d], r_recv.at[d], peer(d)).wait_recv()
    for k in range(z_count):
        y[k] = jnp.dot(
            all_r[k].astype(f32), state, precision=precise, preferred_element_type=f32
        )

    def outgoing(d):
        return (
            remote(y.at[(z + d) % z_count], far.at[z], y_send.at[d], y_recv.at[d], peer(d)),
            remote(pd, far_pd.at[z], p_send.at[d], p_recv.at[d], peer(d)),
        )

    for d in range(1, z_count):
        @pl.when(z + d < z_count)
        def _():
            for copy in outgoing(d):
                copy.start()
    scores = lax.dot_general(
        mine_r[...], writes[...], (((1,), (1,)), ((), ())), preferred_element_type=f32
    )
    causal = (spots >= lanes) & (row_seg == segment)
    half = lax.broadcasted_iota(jnp.int32, (rows, 2 * HEAD_DIM), 1) < HEAD_DIM
    for pair in range(heads // 2):
        mixes = []
        for h in (2 * pair, 2 * pair + 1):
            gaps = row_cum[:, h : h + 1] - cumulated[h : h + 1]
            decay = jnp.where(causal, jnp.exp(jnp.where(causal, gaps, 0.0)), 0.0)
            mixes.append(scores * decay * steps[h : h + 1])
        span = slice(pair * 2 * HEAD_DIM, (pair + 1) * 2 * HEAD_DIM)
        product = jnp.dot(
            jnp.concatenate(mixes, axis=0), values[:, span].astype(f32),
            precision=precise, preferred_element_type=f32,
        )
        mixed[:, span] = jnp.where(half, product[:rows], product[rows:])
    own_values = jnp.dot(pick, values[...], preferred_element_type=f32)
    from_start = jnp.exp(row_cum) * jnp.where(row_seg == 0.0, 1.0, 0.0)
    factors = widen(
        jnp.concatenate([from_start, jnp.broadcast_to(skip_ref[q], (8, heads))], axis=0)
    )
    gate = jax.nn.silu(gate_ref[...].astype(f32))
    carried[...] = jnp.zeros((rows, width), f32)
    for d in range(z_count - 1, 0, -1):
        @pl.when(z - d >= 0)
        def _():
            k = z - d + jnp.where(z - d < 0, z_count, 0)
            here, there = far.at[k], far_pd.at[k]
            remote(here, here, y_send.at[d], y_recv.at[d], peer(d)).wait_recv()
            remote(there, there, p_send.at[d], p_recv.at[d], peer(d)).wait_recv()
            carried[...] = carried[...] * far_pd[k][0:1] + far[k]
    gated = (
        mixed[...] + carried[...] * factors[:rows] + factors[rows : rows + 1] * own_values
    ) * gate
    scale = lax.rsqrt(jnp.mean(gated * gated, axis=1, keepdims=True) + epsilon)
    out[...] = (gated * scale * gain_ref[:, wide]).astype(bf16)
    for copy in sent:
        copy.wait_send()
    for d in range(1, z_count):
        @pl.when(z + d < z_count)
        def _():
            for copy in outgoing(d):
                copy.wait_send()


def middle(xs, x_edge, ss, s_edge, keeps, steps, flags, spots, gate, taps_x, taps_s, rate, skip, gain,
           q_count, z_count):
    f32, bf16 = jnp.float32, jnp.bfloat16
    tokens = steps.shape[0] * steps.shape[2]
    rows, width = gate.shape
    operands = (
        xs, x_edge, ss, s_edge, keeps, steps, flags, spots, gate, taps_x, taps_s, rate, skip, gain
    )
    run, extra = staged(
        functools.partial(mid_kernel, q_count, z_count), (), len(operands), operands
    )
    dma, vmem = pltpu.SemaphoreType.DMA, pltpu.VMEM
    return pl.pallas_call(
        run,
        out_shape=jax.ShapeDtypeStruct((rows, width), bf16),
        in_specs=[ANY] * len(operands),
        out_specs=VMEM,
        scratch_shapes=[
            vmem((EDGE + tokens, width), f32),
            vmem((EDGE + tokens, STATE), f32),
            vmem((tokens, width), bf16),
            vmem((tokens, STATE), bf16),
            vmem((tokens, STATE), bf16),
            vmem((rows, STATE), bf16),
            vmem((z_count, rows, STATE), bf16),
            vmem((z_count, rows, width), f32),
            vmem((z_count, rows, width), f32),
            vmem((8, width), f32),
            vmem((z_count, 8, width), f32),
            vmem((rows, width), f32),
            vmem((rows, width), f32),
        ] + [dma((z_count,))] * 6 + extra,
        compiler_params=pltpu.CompilerParams(
            collective_id=1, has_side_effects=True, vmem_limit_bytes=58 * 1024 * 1024
        ),
    )(*operands)


def tail_kernel(n, tp, q_count, z_count, n_ref, ow_ref, hw_ref, r_ref, g_ref, t_ref, p_ref, out,
                ow, hw, nrm, both, hid, feat, logit, stat, every,
                own, tp_send, tp_recv, st_send, st_recv, *gather_sems):
    c, t = lax.axis_index("ctx"), lax.axis_index("tp")
    z, q = c // q_count, c % q_count
    total = n * tp
    me = c * tp + t
    get_ow = pltpu.make_async_copy(ow_ref, ow, own.at[0])
    get_hw = pltpu.make_async_copy(hw_ref, hw, own.at[1])
    barrier = pltpu.get_barrier_semaphore()

    def device(k):
        return (k // tp, k % tp)

    def hello(d, carry):
        pl.semaphore_signal(
            barrier, inc=1, device_id=device((me + d) % total), device_id_type=MESH
        )
        return carry

    lax.fori_loop(1, total, hello, 0)
    get_ow.start()
    get_hw.start()
    pl.semaphore_wait(barrier, total - 1)
    core_n = 2 if q_count % 2 == 0 else 1
    x_n = q_count // core_n
    x, core = q // core_n, q % core_n

    def at_x(k):
        return (z * q_count + k * core_n + core, t)

    at_core = (z * q_count + x * core_n + (core_n - 1) - core, t)

    def gathered(slot, mine, sems):
        z_send, z_recv, x_send, x_recv, c_send, c_recv = sems
        sent = []

        def push(copy):
            copy.start()
            sent.append(copy)

        def to_x(ref, dst, d):
            for e in range(1, x_n):
                push(remote(ref, dst, x_send.at[e - 1, d], x_recv.at[e - 1, d], at_x((x + e) % x_n)))

        def to_core(ref, dst, e, d):
            if core_n > 1:
                push(remote(ref, dst, c_send.at[e, d], c_recv.at[e, d], at_core))

        home = slot(q, z)
        for d in range(1, z_count):
            push(remote(mine, home, z_send.at[d], z_recv.at[d], (((z + d) % z_count) * q_count + q, t)))
        to_x(mine, home, 0)
        to_core(mine, home, 0, 0)
        for d in range(z_count):
            k = (z + z_count - d) % z_count
            if d:
                here = slot(q, k)
                remote(here, here, z_send.at[d], z_recv.at[d], at_core).wait_recv()
                to_x(here, here, d)
                to_core(here, here, 0, d)
            for e in range(1, x_n):
                here = slot(((x + x_n - e) % x_n) * core_n + core, k)
                remote(here, here, x_send.at[e - 1, d], x_recv.at[e - 1, d], at_core).wait_recv()
                to_core(here, here, e, d)
        if core_n > 1:
            for d in range(z_count):
                k = (z + z_count - d) % z_count
                for e in range(x_n):
                    here = slot(((x + x_n - e) % x_n) * core_n + 1 - core, k)
                    remote(here, here, c_send.at[e, d], c_recv.at[e, d], at_core).wait_recv()
        return sent

    rows = n_ref.shape[0]
    width = n_ref.shape[1]

    def normed_slot(a, b):
        return nrm.at[a, b]

    pending = gathered(normed_slot, n_ref, gather_sems[:6])
    nrm[q, z] = n_ref[...]
    get_ow.wait()
    partial = jnp.zeros(both.shape[1:], jnp.float32)
    for k in range(q_count):
        partial = partial + jnp.dot(
            nrm[k].reshape(z_count * rows, width),
            ow[k * width : (k + 1) * width, :],
            preferred_element_type=jnp.float32,
        )
    both[t] = partial
    tp_copies = []
    for d in range(1, tp):
        copy = remote(both.at[t], both.at[t], tp_send.at[d], tp_recv.at[d], (c, (t + d) % tp))
        copy.start()
        tp_copies.append(copy)
    for d in range(1, tp):
        here = both.at[(t + tp - d) % tp]
        remote(here, here, tp_send.at[d], tp_recv.at[d], (c, (t + d) % tp)).wait_recv()
    summed = both[0]
    for k in range(1, tp):
        summed = summed + both[k]
    hid[q, z] = (r_ref[...].astype(jnp.float32) + summed).astype(jnp.bfloat16)

    def hidden_slot(a, b):
        return hid.at[a, b]

    pending = pending + tp_copies + gathered(hidden_slot, hid.at[q, z], gather_sems[6:])
    block = hid.shape[3]
    all_rows = hid.shape[2]
    squares = jnp.zeros((all_rows, 1), jnp.float32)
    for k in range(z_count):
        for a in range(q_count):
            piece = hid[a, k].astype(jnp.float32)
            squares = squares + jnp.sum(piece * piece, axis=1, keepdims=True)
    inverse = lax.rsqrt(squares / (n * block) + epsilon)
    for k in range(z_count):
        for a in range(q_count):
            first = (k * q_count + a) * block
            span = slice(first, first + block)
            feat[:, span] = (
                hid[a, k].astype(jnp.float32) * inverse * g_ref[:, span]
            ).astype(jnp.bfloat16)
    get_hw.wait()
    vocab = hw.shape[1]
    tile = min(256, vocab)

    def one_tile(i, carry):
        cols = pl.ds(pl.multiple_of(i * tile, 128), tile)
        logit[:, cols] = jnp.dot(feat[...], hw[:, cols], preferred_element_type=jnp.float32)
        return carry

    lax.fori_loop(0, vocab // tile, one_tile, 0)
    values = logit[...]
    top = jnp.max(values, axis=1, keepdims=True)
    added = jnp.sum(jnp.exp(values - top), axis=1, keepdims=True)
    column = t_ref[...] - me * vocab
    places = lax.broadcasted_iota(jnp.int32, values.shape, 1)
    hit = jnp.sum(jnp.where(places == column, values, 0.0), axis=1, keepdims=True)
    lane = lax.broadcasted_iota(jnp.int32, (all_rows, 128), 1)
    packed = jnp.where(lane == 0, top, jnp.where(lane == 1, added, jnp.where(lane == 2, hit, 0.0)))
    turned = packed.T[:8]
    stat[...] = turned

    def go(d, carry):
        remote(
            stat, every.at[me], st_send.at[d], st_recv.at[d], device((me + d) % total)
        ).start()
        return carry

    lax.fori_loop(1, total, go, 0)
    every[me] = turned

    def done(d, carry):
        here = every.at[(me + total - d) % total]
        copy = remote(stat, here, st_send.at[d], st_recv.at[d], device((me + d) % total))
        copy.wait_send()
        copy.wait_recv()
        return carry

    lax.fori_loop(1, total, done, 0)
    for copy in pending:
        copy.wait_send()
    found = every[...]
    tops = found[:, 0, :]
    row_top = jnp.max(tops, axis=0, keepdims=True)
    full = jnp.sum(found[:, 1, :] * jnp.exp(tops - row_top), axis=0, keepdims=True)
    picked = jnp.sum(found[:, 2, :], axis=0, keepdims=True)
    log_prob = picked - row_top - jnp.log(full)
    out[0:1, :] = log_prob
    out[1:2, :] = 0.5 * jnp.square(log_prob - p_ref[...])


def tail(normed, out_weight, head_weight, res, gain, targets, policy, n, tp, q_count, z_count):
    dma = pltpu.SemaphoreType.DMA
    total = n * tp
    rows, width = normed.shape
    all_rows = z_count * rows
    block = out_weight.shape[1]
    core_n = 2 if q_count % 2 == 0 else 1
    x_n = q_count // core_n
    vmem = pltpu.VMEM
    bf16, f32 = jnp.bfloat16, jnp.float32
    e_n = max(x_n - 1, 1)
    sems = [
        dma((z_count,)), dma((z_count,)), dma((e_n, z_count)), dma((e_n, z_count)),
        dma((x_n, z_count)), dma((x_n, z_count)),
    ]
    operands = (
        normed, out_weight, head_weight, res, gain[None], targets[:, None], policy[None]
    )
    run, extra = staged(
        functools.partial(tail_kernel, n, tp, q_count, z_count), (1, 2), len(operands),
        operands[:1] + operands[3:],
    )
    result = pl.pallas_call(
        run,
        out_shape=jax.ShapeDtypeStruct((2, all_rows), f32),
        in_specs=[ANY] * len(operands),
        out_specs=VMEM,
        scratch_shapes=[
            vmem(out_weight.shape, bf16),
            vmem(head_weight.shape, bf16),
            vmem((q_count, z_count, rows, width), bf16),
            vmem((tp, all_rows, block), f32),
            vmem((q_count, z_count, all_rows, block), bf16),
            vmem((all_rows, n * block), bf16),
            vmem((all_rows, head_weight.shape[1]), f32),
            vmem((8, all_rows), f32),
            vmem((total, 8, all_rows), f32),
            dma((2,)), dma((tp,)), dma((tp,)), dma((total,)), dma((total,)),
        ] + sems + sems + extra,
        compiler_params=pltpu.CompilerParams(
            collective_id=3, has_side_effects=True, vmem_limit_bytes=58 * 1024 * 1024
        ),
    )(*operands)
    return result[0], result[1]


def body(
    inner_input,
    gate_input,
    state_inputs,
    step_size,
    resets,
    decay_rate,
    skip_gain,
    conv_inner,
    conv_state,
    norm_gain,
    out_weight,
    residual,
    final_gain,
    head_weight,
    scored,
    targets,
    policy_logprob,
):
    f32 = jnp.float32
    n, tp = lax.axis_size("ctx"), lax.axis_size("tp")
    c, t = lax.axis_index("ctx"), lax.axis_index("tp")
    taps = conv_inner.shape[0]
    rows_here = inner_input.shape[0]
    q_count = state_inputs.shape[2] // STATE
    z_count = n // q_count
    z, q = c // q_count, c % q_count
    picked_rows = scored.shape[0]
    local_rows = scored - c * rows_here
    here = jnp.arange(rows_here, dtype=jnp.int32)
    pick = (local_rows[:, None] == here[None, :]).astype(jnp.bfloat16)
    gate_rows = jnp.dot(pick, gate_input, preferred_element_type=f32).astype(jnp.bfloat16)
    res_rows = jnp.dot(pick, residual, preferred_element_type=f32).astype(jnp.bfloat16)
    meta = jnp.zeros((8, rows_here), f32)
    meta = meta.at[0].set(resets.astype(f32))
    meta = meta.at[1, :picked_rows].set(local_rows.astype(f32))
    xs, ss, ds, gs, ms, x_edge, s_edge, m_edge, res_all = spread(
        n, tp, q_count, inner_input, state_inputs, step_size, gate_rows, meta, res_rows
    )
    tokens = q_count * rows_here
    width = xs.shape[2]
    heads = ds.shape[1]
    rows = q_count * picked_rows
    gate = gs.reshape(rows, width)
    flags = ms[:, 0].reshape(tokens)
    spots = ms[:, 1, :picked_rows] + (jnp.arange(q_count) * rows_here).astype(f32)[:, None]
    spots = spots.reshape(rows, 1).astype(jnp.int32)
    margin = taps - 1
    f_tail = jnp.where(z > 0, m_edge[0, rows_here - margin :], 0.0)
    clear = 1.0 - jnp.concatenate([f_tail, flags])
    keeping = [jnp.ones((tokens,), f32)]
    for offset in range(1, taps):
        keeping.append(keeping[-1] * clear[margin - offset + 1 : margin - offset + 1 + tokens])
    keeps = jnp.pad(jnp.stack(keeping), ((0, -taps % 8), (0, 0)))
    normed = middle(
        xs, x_edge, ss, s_edge, keeps, ds, jnp.broadcast_to(flags[None], (8, tokens)), spots, gate,
        conv_inner, conv_state, decay_rate.reshape(q_count, heads, 1),
        skip_gain.reshape(q_count, 1, heads), norm_gain[None], q_count, z_count,
    )
    res = res_all.reshape(z_count * rows, -1)
    return tail(
        normed, out_weight, head_weight, res, final_gain, targets, policy_logprob,
        n, tp, q_count, z_count,
    )


def solution(mesh):
    return jax.shard_map(
        body,
        mesh=mesh,
        in_specs=(
            P("ctx", "tp"),
            P("ctx", "tp"),
            P(None, "ctx", "tp"),
            P("tp", "ctx"),
            P("ctx"),
            P("tp"),
            P("tp"),
            P(None, "tp"),
            P(None, None, "tp"),
            P("tp"),
            P("tp", "ctx"),
            P("ctx", "tp"),
            P(),
            P(None, ("ctx", "tp")),
            P("ctx"),
            P(),
            P(),
        ),
        out_specs=(P(), P()),
        check_vma=False,
    )
```
